768 devices in a mesh: dp: 16 (over y, core), expert: 48 (over z, x).
Axes of the slice: x: 4, y: 8, z: 12, core: 2. Of those that a mesh axis runs over, the one named last changes fastest.
Arguments:
- tokens: bfloat16 [98304, 3584], P(('dp', 'expert')), may hold values from -6 to 6
- route_weight: float32 [98304], P(('dp', 'expert')), may hold values from 0.1 to 1
- cotangent: bfloat16 [98304, 1024], P(('dp', 'expert')), may hold values from -6 to 6
- slot_ids: int32 [98304], P(('dp', 'expert')), may hold values from 0 to 47, as said below
- placement: int32 [48], replicated, may hold values from 0 to 39, as said below
- weight: bfloat16 [48, 3584, 1024], P('expert'), as said below
- momentum: bfloat16 [48, 3584, 1024], P('expert', 'dp'), as said below
Outputs:
- expert_out: bfloat16 [98304, 1024], P(('dp', 'expert'))
- token_grad: bfloat16 [98304, 3584], P(('dp', 'expert'))
- new_weight: bfloat16 [48, 3584, 1024], P('expert', 'dp')
- new_momentum: bfloat16 [48, 3584, 1024], P('expert', 'dp')
The draws below stay inside these ranges and needn't reach their ends.
Inputs may be any that keep to these rules, and one draw needn't show every extreme that they name: `slot_ids`: one device's 128 tokens (an aligned block) send at most 3 tokens to one slot; in each group of 48 consecutive blocks some slot gets exactly 3 from every block. `placement`: slots j and j + 24 carry the same number for exactly 8 values of j below 24; all other slots carry distinct numbers, and every number is used. `weight`: slots with equal placement numbers hold equal matrices. `momentum`: slots with equal placement numbers hold equal matrices.
All inputs are finite; a program needn't handle non-finite values.
Results may differ from the reference program's by a relative error of at most 0.018.
Values may be sent and summed in bfloat16 or wider, within the bound.
A program may use at most 64 MiB of HBM per device.

```python
import jax
import jax.numpy as jnp
from jax import lax

D = 3584
F = 1024
TOK_DEV = 128
CAP = 3
HOT = 8
TOKENS = 98304
N_DP = 16
N_EXPERT = 48


def layout_table(key):
    base_key = jax.random.fold_in(key, 101)
    pairs = N_EXPERT // 2
    order = jax.random.permutation(jax.random.fold_in(base_key, 1), pairs - 2)
    middle = (order < HOT - 2).astype(jnp.int32)
    edge = jnp.ones((1,), jnp.int32)
    hot_pair = jnp.concatenate([edge, middle, edge])
    units = 2 - hot_pair
    start = jnp.cumsum(units) - units
    labels = jnp.concatenate([start, start + 1 - hot_pair])
    relabel = jax.random.permutation(jax.random.fold_in(base_key, 2), N_EXPERT - HOT)
    return (relabel[labels].astype(jnp.int32), jnp.concatenate([hot_pair, hot_pair]))


def source_slot(key):
    hot_flags = layout_table(key)[1]
    slots = jnp.arange(N_EXPERT, dtype=jnp.int32)
    upper = (slots >= N_EXPERT // 2) & (hot_flags == 1)
    return jnp.where(upper, slots - N_EXPERT // 2, slots)


def draw_placement(key, part):
    return layout_table(key)[0]


def draw_weight(key, part):
    inner = jax.random.fold_in(key, 7)
    values = jax.random.normal(inner, (N_EXPERT, D, F), jnp.float32)
    values = values * D ** (-0.5)
    return values[source_slot(key)].astype(jnp.bfloat16)


def draw_momentum(key, part):
    inner = jax.random.fold_in(key, 9)
    values = jax.random.normal(inner, (N_EXPERT, D, F), jnp.float32) * 10.0
    return values[source_slot(key)].astype(jnp.bfloat16)


def draw_slot_ids(key, part):
    blocks = TOKENS // TOK_DEV
    positions = N_EXPERT * CAP
    full_slot = jax.random.randint(jax.random.fold_in(key, 5), (blocks // N_EXPERT,), 0, N_EXPERT)
    block_full = jnp.repeat(full_slot, N_EXPERT)
    block_keys = jax.random.split(jax.random.fold_in(key, 6), blocks)

    def one_block(block_key, chosen_full):
        first_key, second_key = jax.random.split(block_key)
        priority = jax.random.permutation(first_key, positions)
        places = jnp.arange(positions, dtype=jnp.int32)
        score = jnp.where(places // CAP == chosen_full, -1 - places, priority)
        ordered = jnp.argsort(score)
        picked = (ordered[:TOK_DEV] // CAP).astype(jnp.int32)
        return picked[jax.random.permutation(second_key, TOK_DEV)]
    return jax.vmap(one_block)(block_keys, block_full).reshape(-1).astype(jnp.int32)


def shard_levels(key, extent, cuts, least, largest):
    def one(dim, parts):
        steps = jax.random.uniform(jax.random.fold_in(jax.random.fold_in(key, 6), dim), (parts,), jnp.float32, least / len(cuts), largest / len(cuts))
        return jnp.repeat(jnp.exp(steps), extent[dim] // parts).reshape((-1,) + (1,) * (len(extent) - dim - 1))

    loudness = one(*cuts[0])
    for cut in cuts[1:]:
        loudness = loudness * one(*cut)
    return loudness


def gaussian(own_key, dims, scale, limit, pieces=(), held_as=jnp.bfloat16):
    values = jax.random.normal(own_key, dims, jnp.float32) * scale
    if len(pieces) > 0:
        values = shard_levels(own_key, dims, pieces, -0.22, 0.18) * values
    return jnp.clip(values, min=-limit, max=limit).astype(held_as)


def setup_inputs(seed: int = 0) -> dict:
    seeds = jax.random.split(jax.random.key(seed), 8)
    tokens = gaussian(seeds[0], (TOKENS, D), 1.0, 6.0, ((0, 768),))
    route_weight = jnp.clip(0.1 + 0.9 * jax.random.uniform(seeds[1], (TOKENS,), jnp.float32) ** shard_levels(seeds[1], (TOKENS,), ((0, 768),), -0.2, 0.2), 0.1, 1.0)
    cotangent = gaussian(seeds[2], (TOKENS, F), 1.0, 6.0, ((0, 768),))
    slot_ids = draw_slot_ids(jax.random.fold_in(seeds[7], 71), 0)
    placement = draw_placement(jax.random.fold_in(seeds[7], 71), 0)
    weight = draw_weight(jax.random.fold_in(seeds[7], 71), 0)
    momentum = draw_momentum(jax.random.fold_in(seeds[7], 71), 0)
    return {"tokens": tokens, "route_weight": route_weight, "cotangent": cotangent, "slot_ids": slot_ids, "placement": placement, "weight": weight, "momentum": momentum}


learning_rate = 0.004
decay_rate = 0.9


def reference(tokens, route_weight, cotangent, slot_ids, placement, weight, momentum):
    n_blocks = TOKENS // TOK_DEV
    slot_rows = N_EXPERT * CAP
    blocked = slot_ids.reshape(n_blocks, TOK_DEV)
    onehot = (blocked[:, :, None] == jnp.arange(N_EXPERT, dtype=jnp.int32)[None, None, :]).astype(jnp.int32)
    ranks = jnp.sum((jnp.cumsum(onehot, axis=1) - 1) * onehot, axis=2).astype(jnp.int32)
    block_ids = jnp.arange(n_blocks, dtype=jnp.int32)[:, None]
    group = block_ids // N_EXPERT
    source = block_ids % N_EXPERT
    position = ((((blocked * N_DP + group) * N_EXPERT + source) * CAP) + ranks).reshape(-1).astype(jnp.int32)
    all_rows = N_EXPERT * N_DP * slot_rows
    x_buf = jnp.zeros((all_rows, D), jnp.bfloat16).at[position].set(tokens).reshape(N_EXPERT, N_DP, slot_rows, D)
    scaled = (route_weight[:, None] * cotangent.astype(jnp.float32)).astype(jnp.bfloat16)
    g_buf = jnp.zeros((all_rows, F), jnp.bfloat16).at[position].set(scaled).reshape(N_EXPERT, N_DP, slot_rows, F)

    def per_slot(slot):
        rows_x = x_buf[slot].astype(jnp.float32)
        rows_g = g_buf[slot].astype(jnp.float32)
        matrix = weight[slot].astype(jnp.float32)
        preact = jnp.einsum("nrd,df->nrf", rows_x, matrix)
        sigma = jax.nn.sigmoid(preact)
        act = (preact * sigma).astype(jnp.bfloat16)
        grad_pre = (rows_g * sigma * (1.0 + preact * (1.0 - sigma))).astype(jnp.bfloat16)
        back = jnp.einsum("nrf,df->nrd", grad_pre.astype(jnp.float32), matrix).astype(jnp.bfloat16)
        terms = jnp.einsum("nrd,nrf->ndf", rows_x, grad_pre.astype(jnp.float32))
        terms = lax.optimization_barrier(terms.astype(jnp.bfloat16)).astype(jnp.float32)
        reduced = jnp.sum(terms, axis=0).astype(jnp.bfloat16)
        return act, back, reduced

    act_all, back_all, reduced = lax.map(per_slot, jnp.arange(N_EXPERT, dtype=jnp.int32))
    act_rows = act_all.reshape(all_rows, F)[position]
    expert_out = (route_weight[:, None] * act_rows.astype(jnp.float32)).astype(jnp.bfloat16)
    token_grad = back_all.reshape(all_rows, D)[position]
    half = N_EXPERT // 2
    partner = jnp.roll(reduced, half, axis=0)
    partner_label = jnp.roll(placement, half, axis=0)
    same = (placement == partner_label)[:, None, None]
    total = reduced.astype(jnp.float32) + jnp.where(same, partner.astype(jnp.float32), jnp.float32(0.0))
    new_momentum = (decay_rate * momentum.astype(jnp.float32) + total).astype(jnp.bfloat16)
    new_weight = (weight.astype(jnp.float32) - learning_rate * new_momentum.astype(jnp.float32)).astype(jnp.bfloat16)
    return expert_out, token_grad, new_weight, new_momentum
```

```python
import functools

import jax
import jax.numpy as jnp
from jax import lax
from jax.experimental import pallas as pl
from jax.experimental.pallas import tpu as pltpu
from jax.sharding import PartitionSpec as P

LEARNING_RATE = 0.004
DECAY_RATE = 0.9
CAP = 3
QUARTERS = 4
MESH = pl.DeviceIdType.MESH
F32, BF16 = jnp.float32, jnp.bfloat16


def dot(a, b, dims=((1,), (0,))):
    return lax.dot_general(a, b, (dims, ((), ())), preferred_element_type=F32)


def iota(shape, axis):
    return lax.broadcasted_iota(jnp.int32, shape, axis)


class Plan:
    def __init__(self, n_dp, n_slots):
        self.nz, self.nx = (12, 4) if n_slots == 48 else (n_slots // 2, 2)
        self.ny = n_dp // 2
        self.n_slots, self.n_dp = n_slots, n_dp
        self.dp, self.me = lax.axis_index("dp"), lax.axis_index("expert")
        self.y, self.core = self.dp // 2, self.dp % 2
        self.z, self.x = self.me // self.nx, self.me % self.nx
        self.sign = 1 - 2 * self.core

    def shift(self, k):
        f = self.nz - 1 - k // self.nx
        dz = (f % 2) * ((f + 1) // 2) + (1 - f % 2) * (self.nz - f // 2)
        dx = self.nx - 1 - k % self.nx
        return dz, dx

    def peer(self, k, way):
        dz, dx = self.shift(k)
        z = (self.z + way * self.sign * dz + 2 * self.nz) % self.nz
        x = (self.x + way * self.sign * dx + 2 * self.nx) % self.nx
        return self.dp, z * self.nx + x

    def visit(self, slot):
        zs, xs = slot // self.nx, slot % self.nx
        dz = (self.sign * (zs - self.z) + 2 * self.nz) % self.nz
        dx = (self.sign * (xs - self.x) + 2 * self.nx) % self.nx
        f = jnp.where(dz == 0, 0, jnp.where(dz <= self.nz // 2, 2 * dz - 1, 2 * (self.nz - dz)))
        return (self.nz - 1 - f) * self.nx + (self.nx - 1 - dx)


def body(
    cfg,
    slot_hbm, rw_hbm, tok_hbm, cot_hbm, w_hbm,
    eo_hbm, tg_hbm, red_hbm, pbuf,
    slot_ref, rw_ref, tok_ref, cot_ref, eo_ref, tg_ref,
    wv, stk, send, recv, bsend, brecv, xbuf, gbuf, gpbuf, actbuf, dw, pr, rbuf, red,
    isem, wsem, osem, ssem, rsem, bssem, brsem, prs, prr, rss, rsr, ps, prv,
):
    plan = Plan(cfg["n_dp"], cfg["n_slots"])
    n_slots, ny = plan.n_slots, plan.ny
    tok, d = tok_ref.shape
    f = cot_ref.shape[1]
    dq, fq = d // QUARTERS, f // QUARTERS
    rows = n_slots * CAP
    chunks = cfg["chunks"]
    ft = cfg["ftile"]
    sub = dw.shape[1]

    barrier = pltpu.get_barrier_semaphore()

    def greet(k, c):
        pl.semaphore_signal(barrier, inc=1, device_id=plan.peer(k, 1), device_id_type=MESH)
        return c

    lax.fori_loop(0, n_slots - 1, greet, 0)
    up = (((plan.y + 1) % ny) * 2 + plan.core, plan.me)
    down = (((plan.y + ny - 1) % ny) * 2 + plan.core, plan.me)
    mate = (plan.y * 2 + 1 - plan.core, plan.me)
    for dev in (up, down, mate):
        pl.semaphore_signal(barrier, inc=1, device_id=dev, device_id_type=MESH)

    loads = [
        pltpu.make_async_copy(a, b, isem.at[i])
        for i, (a, b) in enumerate(
            ((slot_hbm, slot_ref), (rw_hbm, rw_ref), (tok_hbm, tok_ref), (cot_hbm, cot_ref)))
    ]
    for cp in loads:
        cp.start()
    w_copy = pltpu.make_async_copy(w_hbm, wv, wsem)
    w_copy.start()
    for cp in loads[:2]:
        cp.wait()

    srow = slot_ref[...]
    hot = (iota((n_slots, tok), 0) == srow).astype(F32)
    tri = (iota((tok, tok), 0) <= iota((tok, tok), 1)).astype(BF16)
    rank = jnp.sum(hot * (dot(hot.astype(BF16), tri) - 1.0), axis=0, keepdims=True)
    place_row = (plan.visit(srow) * CAP + rank.astype(jnp.int32)) * QUARTERS
    diag = iota((tok, tok), 0) == iota((tok, tok), 1)
    upright = lambda row: jnp.sum(jnp.where(diag, row, 0.0), axis=1, keepdims=True)
    place_col = upright(place_row.astype(F32)).astype(jnp.int32)
    rw = upright(rw_ref[...])
    for cp in loads[2:]:
        cp.wait()
    for q in range(QUARTERS):
        stk[q * tok:(q + 1) * tok, :dq] = tok_ref[:, q * dq:(q + 1) * dq]
        stk[q * tok:(q + 1) * tok, dq:] = (rw * cot_ref[:, q * fq:(q + 1) * fq].astype(F32)).astype(BF16)
    want = jnp.concatenate([place_row + q for q in range(QUARTERS)], axis=1)
    pick = jnp.where(iota((rows * QUARTERS, QUARTERS * tok), 0) == want, 1.0, 0.0).astype(BF16)
    packed = dot(pick, stk[:QUARTERS * tok]).astype(BF16).reshape(rows, QUARTERS, dq + fq)
    send[...] = packed
    recv[rows - CAP:] = packed[rows - CAP:]

    pl.semaphore_wait(barrier, n_slots - 1 + 3)

    def slab(ref, k):
        return ref.at[pl.ds(k * CAP, CAP)]

    for c, (k0, k1) in enumerate(chunks):
        def go(k, carry, c=c):
            pltpu.make_async_remote_copy(
                slab(send, k), slab(recv, k), ssem, rsem.at[c],
                device_id=plan.peer(k, 1), device_id_type=MESH).start()
            return carry

        lax.fori_loop(k0, min(k1, n_slots - 1), go, 0)

    def all_of(src, dst, s, r, k0, k1):
        span = pl.ds(k0 * CAP, (min(k1, n_slots - 1) - k0) * CAP)
        return pltpu.make_async_remote_copy(src.at[span], dst.at[span], s, r, device_id=mate, device_id_type=MESH)

    def give_back(k0, k1):
        def back(k, carry):
            pltpu.make_async_remote_copy(
                slab(bsend, k), slab(brecv, k), bssem, brsem,
                device_id=plan.peer(k, -1), device_id_type=MESH).start()
            return carry

        lax.fori_loop(k0, min(k1, n_slots - 1), back, 0)

    for c, (k0, k1) in enumerate(chunks):
        m = (k1 - k0) * CAP
        r0 = k0 * CAP
        all_of(send, recv, ssem, rsem.at[c], k0, k1).wait_recv()
        if c == 0:
            w_copy.wait()
        else:
            give_back(*chunks[c - 1])
        got = recv[r0:r0 + m].reshape(m * QUARTERS, dq + fq)
        for q in range(QUARTERS):
            shape = (m, m * QUARTERS)
            sel = jnp.where(iota(shape, 0) * QUARTERS + q == iota(shape, 1), 1.0, 0.0).astype(BF16)
            part = dot(sel, got).astype(BF16)
            xbuf[r0:r0 + m, q * dq:(q + 1) * dq] = part[:, :dq]
            gbuf[r0:r0 + m, q * fq:(q + 1) * fq] = part[:, dq:]
        for n in range(f // ft):
            cols = slice(n * ft, (n + 1) * ft)
            pre = dot(xbuf[r0:r0 + m], wv[:, cols])
            sigma = jax.nn.sigmoid(pre)
            actbuf[r0:r0 + m, cols] = (pre * sigma).astype(BF16)
            gpbuf[r0:r0 + m, cols] = (
                gbuf[r0:r0 + m, cols].astype(F32) * sigma * (1.0 + pre * (1.0 - sigma))).astype(BF16)
        gp = gpbuf[r0:r0 + m]
        for q in range(QUARTERS):
            stk[q * m:(q + 1) * m, :dq] = dot(gp, wv[q * dq:(q + 1) * dq], ((1,), (1,))).astype(BF16)
            stk[q * m:(q + 1) * m, dq:] = actbuf[r0:r0 + m, q * fq:(q + 1) * fq]
        shape = (m * QUARTERS, m * QUARTERS)
        j = iota(shape, 1)
        jq = sum((j >= m * q).astype(jnp.int32) for q in range(1, QUARTERS))
        sel = jnp.where(iota(shape, 0) == (j - jq * m) * QUARTERS + jq, 1.0, 0.0).astype(BF16)
        packed = dot(sel, stk[:m * QUARTERS]).astype(BF16).reshape(m, QUARTERS, dq + fq)
        bsend[r0:r0 + m] = packed
        if k1 == n_slots:
            brecv[rows - CAP:] = packed[m - CAP:]
    give_back(*chunks[-1])

    per = dq // sub
    for q in range(QUARTERS):
        for n in range(f // ft):
            cols = slice(n * ft, (n + 1) * ft)
            term = dot(xbuf[:, q * dq:(q + 1) * dq], gpbuf[:, cols], ((0,), (0,)))
            dw[q * per:(q + 1) * per, :, cols] = term.astype(BF16).reshape(per, sub, ft)

    owner = lambda i, h: (plan.y - i - 1 + 2 * ny) % ny if h == 0 else (plan.y + i + 1) % ny
    unit = lambda o, core, h: (o * 2 + core) * 4 + h * 2
    pairs = []
    for i in range(ny):
        for h in range(2):
            cp = pltpu.make_async_remote_copy(
                dw.at[pl.ds(unit(owner(i, h), 1 - plan.core, h), 2)],
                pr.at[i, h], prs.at[i, h], prr.at[i, h], device_id=mate, device_id_type=MESH)
            cp.start()
            pairs.append(cp)

    hops = {}
    swaps = []
    out_copies = []
    far = (plan.dp, (plan.me + n_slots // 2) % n_slots)
    for i in range(ny):
        for h in range(2):
            pairs[i * 2 + h].wait_recv()
        for s in range(2):
            for h in range(2):
                u = unit(owner(i, h), plan.core, h) + s
                val = dw[u].astype(F32) + pr[i, h, s].astype(F32)
                if i > 0:
                    hops[i - 1, h, s].wait_recv()
                    val = val + rbuf[i - 1, h, s].astype(F32)
                if i < ny - 1:
                    dw[u] = val.astype(BF16)
                    cp = pltpu.make_async_remote_copy(
                        dw.at[u], rbuf.at[i, h, s], rss.at[i, h, s], rsr.at[i, h, s],
                        device_id=up if h == 0 else down, device_id_type=MESH)
                    hops[i, h, s] = cp
                else:
                    red[h * 2 + s] = val.astype(BF16)
                    out_copies.append(pltpu.make_async_copy(red.at[h * 2 + s], red_hbm.at[h * 2 + s], osem.at[h * 2 + s]))
                    out_copies[-1].start()
                    cp = pltpu.make_async_remote_copy(
                        red.at[h * 2 + s], pbuf.at[h * 2 + s], ps.at[h * 2 + s], prv.at[h * 2 + s],
                        device_id=far, device_id_type=MESH)
                    swaps.append(cp)
                cp.start()

    all_of(bsend, brecv, bssem, brsem, 0, n_slots).wait_recv()
    back_rows = brecv[...].reshape(rows * QUARTERS, dq + fq)
    for q in range(QUARTERS):
        sel = jnp.where(iota((tok, rows * QUARTERS), 1) == place_col + q, 1.0, 0.0).astype(BF16)
        mine = dot(sel, back_rows)
        tg_ref[:, q * dq:(q + 1) * dq] = mine[:, :dq].astype(BF16)
        eo_ref[:, q * fq:(q + 1) * fq] = (rw * mine[:, dq:].astype(BF16).astype(F32)).astype(BF16)

    for i, (a, b) in enumerate(((eo_ref, eo_hbm), (tg_ref, tg_hbm))):
        out_copies.append(pltpu.make_async_copy(a, b, osem.at[4 + i]))
        out_copies[-1].start()

    all_of(send, recv, ssem, rsem.at[0], 0, n_slots).wait_send()
    all_of(bsend, brecv, bssem, brsem, 0, n_slots).wait_send()
    for cp in pairs:
        cp.wait_send()
    for cp in hops.values():
        cp.wait_send()
    for cp in out_copies:
        cp.wait()
    for cp in swaps:
        cp.wait_send()
    for cp in swaps:
        cp.wait_recv()


def finish(
    n_dp,
    place_ref, eo_in, tg_in, red_in, pbuf_in, w_hbm, mom_hbm,
    eo_out, tg_out, nw_out, nm_out,
    eov, tgv, redv, pbufv, wv, momv, nwv, nmv, isem, osem,
):
    dp, me, n_slots = lax.axis_index("dp"), lax.axis_index("expert"), place_ref.shape[1]
    share, f = momv.shape
    sub = share // 4
    ins = [
        pltpu.make_async_copy(a, b, isem.at[i])
        for i, (a, b) in enumerate((
            (tg_in, tgv), (eo_in, eov), (mom_hbm, momv),
            (w_hbm.at[pl.ds(pl.multiple_of(dp * share, 8), share)], wv), (red_in, redv), (pbuf_in, pbufv)))
    ]
    for cp in ins:
        cp.start()
    outs = [
        pltpu.make_async_copy(a, b, osem.at[i])
        for i, (a, b) in enumerate(((tgv, tg_out), (eov, eo_out), (nwv, nw_out), (nmv, nm_out)))
    ]
    labels = place_ref[...]
    lane = iota(labels.shape, 1)
    label = lambda s: jnp.sum(jnp.where(lane == s, labels, 0).astype(F32), axis=1, keepdims=True)
    same = jnp.where(label(me) == label((me + n_slots // 2) % n_slots), 1.0, 0.0)
    mask = jnp.broadcast_to(same, (sub, f)) > 0.5
    for i in range(2):
        ins[i].wait()
        outs[i].start()
    for cp in ins[2:]:
        cp.wait()
    for p in range(4):
        rs = slice(p * sub, (p + 1) * sub)
        total = redv[p].astype(F32) + jnp.where(mask, pbufv[p].astype(F32), 0.0)
        fresh = (DECAY_RATE * momv[rs].astype(F32) + total).astype(BF16)
        nmv[rs] = fresh
        nwv[rs] = (wv[rs].astype(F32) - LEARNING_RATE * fresh.astype(F32)).astype(BF16)
    for cp in outs[2:]:
        cp.start()
    for cp in outs:
        cp.wait()


CHUNKS = ((0, 24), (24, 48))


def shards(tokens, route_weight, cotangent, slot_ids, placement, weight, momentum):
    n_slots, n_dp = lax.axis_size("expert"), lax.axis_size("dp")
    tok, d = tokens.shape
    f = cotangent.shape[1]
    rows, ny = n_slots * CAP, n_dp // 2
    share = d // n_dp
    sub = share // 4
    dq, fq = d // QUARTERS, f // QUARTERS
    chunks = CHUNKS if n_slots == 48 else ((0, n_slots // 2), (n_slots // 2, n_slots))
    cfg = dict(n_dp=n_dp, n_slots=n_slots, chunks=chunks, ftile=min(f, 256))
    vmem, dma = pltpu.VMEM, pltpu.SemaphoreType.DMA
    on_chip, anywhere = pl.BlockSpec(memory_space=pltpu.VMEM), pl.BlockSpec(memory_space=pl.ANY)
    slabs = (rows, QUARTERS, dq + fq)
    shape = jax.ShapeDtypeStruct
    pieces = shape((4, sub, f), BF16)
    results = (shape((tok, f), BF16), shape((tok, d), BF16), shape((share, f), BF16), shape((share, f), BF16))
    eo, tg, red, partner = pl.pallas_call(
        functools.partial(body, cfg),
        out_shape=results[:2] + (pieces, pieces),
        in_specs=[anywhere] * 5,
        out_specs=(anywhere,) * 4,
        scratch_shapes=[
            vmem((1, tok), jnp.int32), vmem((1, tok), F32),
            vmem((tok, d), BF16), vmem((tok, f), BF16), vmem((tok, f), BF16), vmem((tok, d), BF16),
            vmem((d, f), BF16),
            vmem((QUARTERS * max(rows, tok), dq + fq), BF16),
            vmem(slabs, BF16), vmem(slabs, BF16), vmem(slabs, BF16), vmem(slabs, BF16),
            vmem((rows, d), BF16),
            vmem((rows, f), BF16), vmem((rows, f), BF16), vmem((rows, f), BF16),
            vmem((n_dp * 4, sub, f), BF16),
            vmem((ny, 2, 2, sub, f), BF16),
            vmem((ny - 1, 2, 2, sub, f), BF16),
            vmem((4, sub, f), BF16),
            dma((4,)), dma, dma((6,)), dma, dma((len(chunks),)), dma, dma,
            dma((ny, 2)), dma((ny, 2)),
            dma((ny - 1, 2, 2)), dma((ny - 1, 2, 2)),
            dma((4,)), dma((4,)),
        ],
        compiler_params=pltpu.CompilerParams(
            collective_id=0, has_side_effects=True, vmem_limit_bytes=60 * 1024 * 1024),
    )(slot_ids[None, :], route_weight[None, :], tokens, cotangent, weight[0])
    eo, tg, nw, nm = pl.pallas_call(
        functools.partial(finish, n_dp),
        out_shape=results,
        in_specs=[on_chip] + [anywhere] * 6,
        out_specs=(anywhere,) * 4,
        scratch_shapes=[
            vmem((tok, f), BF16), vmem((tok, d), BF16), vmem((4, sub, f), BF16), vmem((4, sub, f), BF16),
            vmem((share, f), BF16), vmem((share, f), BF16), vmem((share, f), BF16), vmem((share, f), BF16),
            dma((6,)), dma((4,)),
        ],
    )(placement[None, :], eo, tg, red, partner, weight[0], momentum[0])
    return eo, tg, nw[None], nm[None]


def solution(mesh):
    return jax.shard_map(
        shards,
        mesh=mesh,
        in_specs=(
            P(("dp", "expert"), None),
            P(("dp", "expert")),
            P(("dp", "expert"), None),
            P(("dp", "expert")),
            P(),
            P("expert", None, None),
            P("expert", "dp", None),
        ),
        out_specs=(
            P(("dp", "expert"), None),
            P(("dp", "expert"), None),
            P("expert", "dp", None),
            P("expert", "dp", None),
        ),
        check_vma=False,
    )
```

```python
import functools

import jax
import jax.numpy as jnp
from jax import lax
from jax.experimental import pallas as pl
from jax.experimental.pallas import tpu as pltpu
from jax.sharding import PartitionSpec as P

LEARNING_RATE = 0.004
DECAY_RATE = 0.9
CAP = 3
QUARTERS = 4
MESH = pl.DeviceIdType.MESH
F32, BF16 = jnp.float32, jnp.bfloat16


def dot(a, b, dims=((1,), (0,))):
    return lax.dot_general(a, b, (dims, ((), ())), preferred_element_type=F32)


def iota(shape, axis):
    return lax.broadcasted_iota(jnp.int32, shape, axis)


class Plan:
    def __init__(self, n_dp, n_slots):
        self.nz, self.nx = (12, 4) if n_slots == 48 else (n_slots // 2, 2)
        self.ny = n_dp // 2
        self.n_slots, self.n_dp = n_slots, n_dp
        self.dp, self.me = lax.axis_index("dp"), lax.axis_index("expert")
        self.y, self.core = self.dp // 2, self.dp % 2
        self.z, self.x = self.me // self.nx, self.me % self.nx
        self.sign = 1 - 2 * self.core

    def shift(self, k):
        f = self.nz - 1 - k // self.nx
        dz = (f % 2) * ((f + 1) // 2) + (1 - f % 2) * (self.nz - f // 2)
        dx = self.nx - 1 - k % self.nx
        return dz, dx

    def peer(self, k, way):
        dz, dx = self.shift(k)
        z = (self.z + way * self.sign * dz + 2 * self.nz) % self.nz
        x = (self.x + way * self.sign * dx + 2 * self.nx) % self.nx
        return self.dp, z * self.nx + x

    def visit(self, slot):
        zs, xs = slot // self.nx, slot % self.nx
        dz = (self.sign * (zs - self.z) + 2 * self.nz) % self.nz
        dx = (self.sign * (xs - self.x) + 2 * self.nx) % self.nx
        f = jnp.where(dz == 0, 0, jnp.where(dz <= self.nz // 2, 2 * dz - 1, 2 * (self.nz - dz)))
        return (self.nz - 1 - f) * self.nx + (self.nx - 1 - dx)


def body(
    cfg,
    slot_hbm, rw_hbm, tok_hbm, cot_hbm, w_hbm,
    eo_hbm, tg_hbm, red_hbm, pbuf,
    slot_ref, rw_ref, tok_ref, cot_ref, eo_ref, tg_ref,
    wv, stk, send, recv, bsend, brecv, xbuf, gbuf, gpbuf, actbuf, dw, pr, rbuf, red,
    isem, wsem, osem, ssem, rsem, bssem, brsem, prs, prr, rss, rsr, ps, prv,
):
    plan = Plan(cfg["n_dp"], cfg["n_slots"])
    n_slots, ny = plan.n_slots, plan.ny
    tok, d = tok_ref.shape
    f = cot_ref.shape[1]
    dq, fq = d // QUARTERS, f // QUARTERS
    rows = n_slots * CAP
    chunks = cfg["chunks"]
    ft = cfg["ftile"]
    half_rows = dw.shape[2]

    barrier = pltpu.get_barrier_semaphore()

    def greet(k, c):
        pl.semaphore_signal(barrier, inc=1, device_id=plan.peer(k, 1), device_id_type=MESH)
        return c

    lax.fori_loop(0, n_slots - 1, greet, 0)
    up = (((plan.y + 1) % ny) * 2 + plan.core, plan.me)
    down = (((plan.y + ny - 1) % ny) * 2 + plan.core, plan.me)
    mate = (plan.y * 2 + 1 - plan.core, plan.me)
    for dev in (up, down, mate):
        pl.semaphore_signal(barrier, inc=1, device_id=dev, device_id_type=MESH)

    loads = [
        pltpu.make_async_copy(a, b, isem.at[i])
        for i, (a, b) in enumerate(
            ((slot_hbm, slot_ref), (rw_hbm, rw_ref), (tok_hbm, tok_ref), (cot_hbm, cot_ref)))
    ]
    for cp in loads:
        cp.start()
    w_copy = pltpu.make_async_copy(w_hbm, wv, wsem)
    w_copy.start()
    for cp in loads[:2]:
        cp.wait()

    srow = slot_ref[...]
    hot = (iota((n_slots, tok), 0) == srow).astype(F32)
    tri = (iota((tok, tok), 0) <= iota((tok, tok), 1)).astype(BF16)
    rank = jnp.sum(hot * (dot(hot.astype(BF16), tri) - 1.0), axis=0, keepdims=True)
    place_row = (plan.visit(srow) * CAP + rank.astype(jnp.int32)) * QUARTERS
    diag = iota((tok, tok), 0) == iota((tok, tok), 1)
    upright = lambda row: jnp.sum(jnp.where(diag, row, 0.0), axis=1, keepdims=True)
    place_col = upright(place_row.astype(F32)).astype(jnp.int32)
    rw = upright(rw_ref[...])
    for cp in loads[2:]:
        cp.wait()
    for q in range(QUARTERS):
        stk[q * tok:(q + 1) * tok, :dq] = tok_ref[:, q * dq:(q + 1) * dq]
        stk[q * tok:(q + 1) * tok, dq:] = (rw * cot_ref[:, q * fq:(q + 1) * fq].astype(F32)).astype(BF16)
    want = jnp.concatenate([place_row + q for q in range(QUARTERS)], axis=1)
    pick = jnp.where(iota((rows * QUARTERS, QUARTERS * tok), 0) == want, 1.0, 0.0).astype(BF16)
    packed = dot(pick, stk[:QUARTERS * tok]).astype(BF16).reshape(rows, QUARTERS, dq + fq)
    send[...] = packed
    recv[rows - CAP:] = packed[rows - CAP:]

    pl.semaphore_wait(barrier, n_slots - 1 + 3)

    def slab(ref, k):
        return ref.at[pl.ds(k * CAP, CAP)]

    for c, (k0, k1) in enumerate(chunks):
        def go(k, carry, c=c):
            pltpu.make_async_remote_copy(
                slab(send, k), slab(recv, k), ssem, rsem.at[c],
                device_id=plan.peer(k, 1), device_id_type=MESH).start()
            return carry

        lax.fori_loop(k0, min(k1, n_slots - 1), go, 0)

    def all_of(src, dst, s, r, k0, k1):
        span = pl.ds(k0 * CAP, (min(k1, n_slots - 1) - k0) * CAP)
        return pltpu.make_async_remote_copy(src.at[span], dst.at[span], s, r, device_id=mate, device_id_type=MESH)

    def forward(c):
        k0, k1 = chunks[c]
        m, r0 = (k1 - k0) * CAP, k0 * CAP
        all_of(send, recv, ssem, rsem.at[c], k0, k1).wait_recv()
        if c == 0:
            w_copy.wait()
        got = recv[r0:r0 + m].reshape(m * QUARTERS, dq + fq)
        for q in range(QUARTERS):
            shape = (m, m * QUARTERS)
            sel = jnp.where(iota(shape, 0) * QUARTERS + q == iota(shape, 1), 1.0, 0.0).astype(BF16)
            part = dot(sel, got).astype(BF16)
            xbuf[r0:r0 + m, q * dq:(q + 1) * dq] = part[:, :dq]
            gbuf[r0:r0 + m, q * fq:(q + 1) * fq] = part[:, dq:]
        for n in range(f // ft):
            cols = slice(n * ft, (n + 1) * ft)
            pre = dot(xbuf[r0:r0 + m], wv[:, cols])
            sigma = jax.nn.sigmoid(pre)
            actbuf[r0:r0 + m, cols] = (pre * sigma).astype(BF16)
            gpbuf[r0:r0 + m, cols] = (
                gbuf[r0:r0 + m, cols].astype(F32) * sigma * (1.0 + pre * (1.0 - sigma))).astype(BF16)

    def give_back(c):
        k0, k1 = chunks[c]
        m, r0 = (k1 - k0) * CAP, k0 * CAP
        gp = gpbuf[r0:r0 + m]
        for q in range(QUARTERS):
            stk[q * m:(q + 1) * m, :dq] = dot(gp, wv[q * dq:(q + 1) * dq], ((1,), (1,))).astype(BF16)
            stk[q * m:(q + 1) * m, dq:] = actbuf[r0:r0 + m, q * fq:(q + 1) * fq]
        shape = (m * QUARTERS, m * QUARTERS)
        j = iota(shape, 1)
        jq = sum((j >= m * q).astype(jnp.int32) for q in range(1, QUARTERS))
        sel = jnp.where(iota(shape, 0) == (j - jq * m) * QUARTERS + jq, 1.0, 0.0).astype(BF16)
        packed = dot(sel, stk[:m * QUARTERS]).astype(BF16).reshape(m, QUARTERS, dq + fq)
        bsend[r0:r0 + m] = packed
        if k1 == n_slots:
            brecv[rows - CAP:] = packed[m - CAP:]

    def start_back(c):
        def back(k, carry):
            pltpu.make_async_remote_copy(
                slab(bsend, k), slab(brecv, k), bssem, brsem,
                device_id=plan.peer(k, -1), device_id_type=MESH).start()
            return carry

        lax.fori_loop(chunks[c][0], min(chunks[c][1], n_slots - 1), back, 0)

    last = len(chunks) - 1
    for c in range(last):
        forward(c)
        give_back(c)
        if EARLY:
            start_back(c)
    forward(last)
    if not EARLY:
        for c in range(last):
            start_back(c)

    groups = f // ft
    per = dq // half_rows
    owner = lambda i, h: (plan.y - i - 1 + 2 * ny) % ny if h == 0 else (plan.y + i + 1) % ny
    unit = lambda o, core, h: (o * 2 + core) * 2 + h
    far = (plan.dp, (plan.me + n_slots // 2) % n_slots)
    pairs, hops, swaps, out_copies = {}, {}, [], []

    def term(g):
        for q in range(QUARTERS):
            part = dot(xbuf[:, q * dq:(q + 1) * dq], gpbuf[:, g * ft:(g + 1) * ft], ((0,), (0,)))
            dw[g, q * per:(q + 1) * per] = part.astype(BF16).reshape(per, half_rows, ft)
        for i in range(ny):
            for h in range(2):
                cp = pltpu.make_async_remote_copy(
                    dw.at[g, unit(owner(i, h), 1 - plan.core, h)], pr.at[g, i, h], prs.at[g, i, h], prr.at[g, i, h],
                    device_id=mate, device_id_type=MESH)
                cp.start()
                pairs[g, i, h] = cp

    def hop(i, g):
        for h in range(2):
            u = unit(owner(i, h), plan.core, h)
            pairs[g, i, h].wait_recv()
            val = dw[g, u].astype(F32) + pr[g, i, h].astype(F32)
            if i > 0:
                hops[i - 1, g, h].wait_recv()
                val = val + rbuf[g, i - 1, h].astype(F32)
            if i < ny - 1:
                dw[g, u] = val.astype(BF16)
                cp = pltpu.make_async_remote_copy(
                    dw.at[g, u], rbuf.at[g, i, h], rss.at[g, i, h], rsr.at[g, i, h],
                    device_id=up if h == 0 else down, device_id_type=MESH)
                hops[i, g, h] = cp
            else:
                red[h, g] = val.astype(BF16)
                out_copies.append(pltpu.make_async_copy(red.at[h, g], red_hbm.at[h, g], osem.at[2 + h * groups + g]))
                out_copies[-1].start()
                cp = pltpu.make_async_remote_copy(
                    red.at[h, g], pbuf.at[h, g], ps.at[h, g], prv.at[h, g], device_id=far, device_id_type=MESH)
                swaps.append(cp)
            cp.start()

    term(0)
    for g in range(1, groups):
        term(g)
        hop(0, g - 1)
    hop(0, groups - 1)
    give_back(last)
    start_back(last)
    for i in range(1, ny):
        for g in range(groups):
            hop(i, g)

    all_of(bsend, brecv, bssem, brsem, 0, n_slots).wait_recv()
    back_rows = brecv[...].reshape(rows * QUARTERS, dq + fq)
    for q in range(QUARTERS):
        sel = jnp.where(iota((tok, rows * QUARTERS), 1) == place_col + q, 1.0, 0.0).astype(BF16)
        mine = dot(sel, back_rows)
        tg_ref[:, q * dq:(q + 1) * dq] = mine[:, :dq].astype(BF16)
        eo_ref[:, q * fq:(q + 1) * fq] = (rw * mine[:, dq:].astype(BF16).astype(F32)).astype(BF16)

    for i, (a, b) in enumerate(((eo_ref, eo_hbm), (tg_ref, tg_hbm))):
        out_copies.append(pltpu.make_async_copy(a, b, osem.at[i]))
        out_copies[-1].start()

    all_of(send, recv, ssem, rsem.at[0], 0, n_slots).wait_send()
    all_of(bsend, brecv, bssem, brsem, 0, n_slots).wait_send()
    for cp in pairs.values():
        cp.wait_send()
    for cp in hops.values():
        cp.wait_send()
    for cp in out_copies:
        cp.wait()
    for cp in swaps:
        cp.wait_send()
    for cp in swaps:
        cp.wait_recv()


def finish(
    n_dp,
    place_ref, eo_in, tg_in, red_in, pbuf_in, w_hbm, mom_hbm,
    eo_out, tg_out, nw_out, nm_out,
    eov, tgv, redv, pbufv, wv, momv, nwv, nmv, isem, tsem, osem,
):
    dp, me, n_slots = lax.axis_index("dp"), lax.axis_index("expert"), place_ref.shape[1]
    _, groups, half, ft = redv.shape
    row0 = dp * 2 * half
    ins = {}
    for h in range(2):
        old = w_hbm.at[pl.ds(pl.multiple_of(row0 + h * half, 8), half)]
        for j, (a, b) in enumerate((
            (red_in.at[h], redv.at[h]), (pbuf_in.at[h], pbufv.at[h]), (mom_hbm.at[pl.ds(h * half, half)], momv.at[h]), (old, wv.at[h]))):
            ins[h, j] = pltpu.make_async_copy(a, b, isem.at[h, j])
            ins[h, j].start()
    whole = [pltpu.make_async_copy(a, b, tsem.at[i]) for i, (a, b) in enumerate(((tg_in, tgv), (eo_in, eov)))]
    for cp in whole:
        cp.start()
    outs = [pltpu.make_async_copy(a, b, osem.at[i]) for i, (a, b) in enumerate(((tgv, tg_out), (eov, eo_out)))]
    labels = place_ref[...]
    lane = iota(labels.shape, 1)
    label = lambda s: jnp.sum(jnp.where(lane == s, labels, 0).astype(F32), axis=1, keepdims=True)
    same = jnp.where(label(me) == label((me + n_slots // 2) % n_slots), 1.0, 0.0)
    mask = jnp.broadcast_to(same, (half, ft)) > 0.5
    for h in range(2):
        for j in range(4):
            ins[h, j].wait()
        for g in range(groups):
            cols = slice(g * ft, (g + 1) * ft)
            total = redv[h, g].astype(F32) + jnp.where(mask, pbufv[h, g].astype(F32), 0.0)
            fresh = (DECAY_RATE * momv[h, :, cols].astype(F32) + total).astype(BF16)
            nmv[h, :, cols] = fresh
            nwv[h, :, cols] = (wv[h, :, cols].astype(F32) - LEARNING_RATE * fresh.astype(F32)).astype(BF16)
        for j, (a, b) in enumerate(((nmv, nm_out), (nwv, nw_out))):
            outs.append(pltpu.make_async_copy(a.at[h], b.at[pl.ds(h * half, half)], osem.at[2 + h * 2 + j]))
            outs[-1].start()
        if h == 0:
            for i in range(2):
                whole[i].wait()
                outs[i].start()
    for cp in outs:
        cp.wait()


EARLY = True
CHUNKS = ((0, 24), (24, 48))


def shards(tokens, route_weight, cotangent, slot_ids, placement, weight, momentum):
    n_slots, n_dp = lax.axis_size("expert"), lax.axis_size("dp")
    tok, d = tokens.shape
    f = cotangent.shape[1]
    rows, ny = n_slots * CAP, n_dp // 2
    share = d // n_dp
    half, ft = share // 2, min(f, 256)
    groups = f // ft
    dq, fq = d // QUARTERS, f // QUARTERS
    chunks = CHUNKS if n_slots == 48 else ((0, n_slots // 2), (n_slots // 2, n_slots))
    cfg = dict(n_dp=n_dp, n_slots=n_slots, chunks=chunks, ftile=ft)
    vmem, dma = pltpu.VMEM, pltpu.SemaphoreType.DMA
    on_chip, anywhere = pl.BlockSpec(memory_space=pltpu.VMEM), pl.BlockSpec(memory_space=pl.ANY)
    slabs = (rows, QUARTERS, dq + fq)
    shape = jax.ShapeDtypeStruct
    pieces = shape((2, groups, half, ft), BF16)
    results = (shape((tok, f), BF16), shape((tok, d), BF16), shape((share, f), BF16), shape((share, f), BF16))
    eo, tg, red, partner = pl.pallas_call(
        functools.partial(body, cfg),
        out_shape=results[:2] + (pieces, pieces),
        in_specs=[anywhere] * 5,
        out_specs=(anywhere,) * 4,
        scratch_shapes=[
            vmem((1, tok), jnp.int32), vmem((1, tok), F32),
            vmem((tok, d), BF16), vmem((tok, f), BF16), vmem((tok, f), BF16), vmem((tok, d), BF16),
            vmem((d, f), BF16),
            vmem((QUARTERS * max(rows, tok), dq + fq), BF16),
            vmem(slabs, BF16), vmem(slabs, BF16), vmem(slabs, BF16), vmem(slabs, BF16),
            vmem((rows, d), BF16),
            vmem((rows, f), BF16), vmem((rows, f), BF16), vmem((rows, f), BF16),
            vmem((groups, n_dp * 2, half, ft), BF16),
            vmem((groups, ny, 2, half, ft), BF16),
            vmem((groups, ny - 1, 2, half, ft), BF16),
            vmem((2, groups, half, ft), BF16),
            dma((4,)), dma, dma((2 + 2 * groups,)), dma, dma((len(chunks),)), dma, dma,
            dma((groups, ny, 2)), dma((groups, ny, 2)),
            dma((groups, ny - 1, 2)), dma((groups, ny - 1, 2)),
            dma((2, groups)), dma((2, groups)),
        ],
        compiler_params=pltpu.CompilerParams(
            collective_id=0, has_side_effects=True, vmem_limit_bytes=60 * 1024 * 1024),
    )(slot_ids[None, :], route_weight[None, :], tokens, cotangent, weight[0])
    eo, tg, nw, nm = pl.pallas_call(
        functools.partial(finish, n_dp),
        out_shape=results,
        in_specs=[on_chip] + [anywhere] * 6,
        out_specs=(anywhere,) * 4,
        scratch_shapes=[
            vmem((tok, f), BF16), vmem((tok, d), BF16), vmem((2, groups, half, ft), BF16), vmem((2, groups, half, ft), BF16),
            vmem((2, half, f), BF16), vmem((2, half, f), BF16), vmem((2, half, f), BF16), vmem((2, half, f), BF16),
            dma((2, 4)), dma((2,)), dma((6,)),
        ],
    )(placement[None, :], eo, tg, red, partner, weight[0], momentum[0])
    return eo, tg, nw[None], nm[None]


def solution(mesh):
    return jax.shard_map(
        shards,
        mesh=mesh,
        in_specs=(
            P(("dp", "expert"), None),
            P(("dp", "expert")),
            P(("dp", "expert"), None),
            P(("dp", "expert")),
            P(),
            P("expert", None, None),
            P("expert", "dp", None),
        ),
        out_specs=(
            P(("dp", "expert"), None),
            P(("dp", "expert"), None),
            P("expert", "dp", None),
            P("expert", "dp", None),
        ),
        check_vma=False,
    )
```

```python
import functools

import jax
import jax.numpy as jnp
from jax import lax
from jax.experimental import pallas as pl
from jax.experimental.pallas import tpu as pltpu
from jax.sharding import PartitionSpec as P

LEARNING_RATE = 0.004
DECAY_RATE = 0.9
CAP = 3
QUARTERS = 4
MESH = pl.DeviceIdType.MESH
F32, BF16 = jnp.float32, jnp.bfloat16


def dot(a, b, dims=((1,), (0,))):
    return lax.dot_general(a, b, (dims, ((), ())), preferred_element_type=F32)


def iota(shape, axis):
    return lax.broadcasted_iota(jnp.int32, shape, axis)


class Plan:
    def __init__(self, n_dp, n_slots):
        self.nz, self.nx = (12, 4) if n_slots == 48 else (n_slots // 2, 2)
        self.ny = n_dp // 2
        self.n_slots, self.n_dp = n_slots, n_dp
        self.dp, self.me = lax.axis_index("dp"), lax.axis_index("expert")
        self.y, self.core = self.dp // 2, self.dp % 2
        self.z, self.x = self.me // self.nx, self.me % self.nx
        self.sign = 1 - 2 * self.core

    def shift(self, k):
        f = self.nz - 1 - k // self.nx
        dz = (f % 2) * ((f + 1) // 2) + (1 - f % 2) * (self.nz - f // 2)
        dx = self.nx - 1 - k % self.nx
        return dz, dx

    def peer(self, k, way):
        dz, dx = self.shift(k)
        z = (self.z + way * self.sign * dz + 2 * self.nz) % self.nz
        x = (self.x + way * self.sign * dx + 2 * self.nx) % self.nx
        return self.dp, z * self.nx + x

    def visit(self, slot):
        zs, xs = slot // self.nx, slot % self.nx
        dz = (self.sign * (zs - self.z) + 2 * self.nz) % self.nz
        dx = (self.sign * (xs - self.x) + 2 * self.nx) % self.nx
        f = jnp.where(dz == 0, 0, jnp.where(dz <= self.nz // 2, 2 * dz - 1, 2 * (self.nz - dz)))
        return (self.nz - 1 - f) * self.nx + (self.nx - 1 - dx)


def body(
    cfg,
    slot_hbm, rw_hbm, place_hbm, tok_hbm, cot_hbm, w_hbm,
    eo_hbm, tg_hbm, red_hbm, pbuf,
    slot_ref, rw_ref, place_ref, tok_ref, cot_ref, eo_ref, tg_ref,
    wv, stk, send, recv, bsend, brecv, xbuf, gbuf, gpbuf, actbuf, dw, pr, rbuf, red, redm,
    isem, wsem, osem, ssem, rsem, bssem, brsem, prs, prr, rss, rsr, ps, prv,
):
    plan = Plan(cfg["n_dp"], cfg["n_slots"])
    n_slots, ny = plan.n_slots, plan.ny
    tok, d = tok_ref.shape
    f = cot_ref.shape[1]
    dq, fq = d // QUARTERS, f // QUARTERS
    rows = n_slots * CAP
    chunks = cfg["chunks"]
    ft = cfg["ftile"]
    half_rows = dw.shape[2]

    barrier = pltpu.get_barrier_semaphore()

    def greet(k, c):
        pl.semaphore_signal(barrier, inc=1, device_id=plan.peer(k, 1), device_id_type=MESH)
        return c

    lax.fori_loop(0, n_slots - 1, greet, 0)
    up = (((plan.y + 1) % ny) * 2 + plan.core, plan.me)
    down = (((plan.y + ny - 1) % ny) * 2 + plan.core, plan.me)
    mate = (plan.y * 2 + 1 - plan.core, plan.me)
    for dev in (up, down, mate):
        pl.semaphore_signal(barrier, inc=1, device_id=dev, device_id_type=MESH)

    loads = [
        pltpu.make_async_copy(a, b, isem.at[i])
        for i, (a, b) in enumerate(
            ((slot_hbm, slot_ref), (rw_hbm, rw_ref), (place_hbm, place_ref), (tok_hbm, tok_ref), (cot_hbm, cot_ref)))
    ]
    for cp in loads:
        cp.start()
    w_copy = pltpu.make_async_copy(w_hbm, wv, wsem)
    w_copy.start()
    for cp in loads[:3]:
        cp.wait()

    srow = slot_ref[...]
    hot = (iota((n_slots, tok), 0) == srow).astype(F32)
    tri = (iota((tok, tok), 0) <= iota((tok, tok), 1)).astype(BF16)
    rank = jnp.sum(hot * (dot(hot.astype(BF16), tri) - 1.0), axis=0, keepdims=True)
    place_row = (plan.visit(srow) * CAP + rank.astype(jnp.int32)) * QUARTERS
    diag = iota((tok, tok), 0) == iota((tok, tok), 1)
    upright = lambda row: jnp.sum(jnp.where(diag, row, 0.0), axis=1, keepdims=True)
    place_col = upright(place_row.astype(F32)).astype(jnp.int32)
    rw = upright(rw_ref[...])
    for cp in loads[3:]:
        cp.wait()
    for q in range(QUARTERS):
        stk[q * tok:(q + 1) * tok, :dq] = tok_ref[:, q * dq:(q + 1) * dq]
        stk[q * tok:(q + 1) * tok, dq:] = (rw * cot_ref[:, q * fq:(q + 1) * fq].astype(F32)).astype(BF16)
    want = jnp.concatenate([place_row + q for q in range(QUARTERS)], axis=1)
    pick = jnp.where(iota((rows * QUARTERS, QUARTERS * tok), 0) == want, 1.0, 0.0).astype(BF16)
    packed = dot(pick, stk[:QUARTERS * tok]).astype(BF16).reshape(rows, QUARTERS, dq + fq)
    send[...] = packed
    recv[rows - CAP:] = packed[rows - CAP:]

    pl.semaphore_wait(barrier, n_slots - 1 + 3)

    def slab(ref, k):
        return ref.at[pl.ds(k * CAP, CAP)]

    for c, (k0, k1) in enumerate(chunks):
        def go(k, carry, c=c):
            pltpu.make_async_remote_copy(
                slab(send, k), slab(recv, k), ssem, rsem.at[c],
                device_id=plan.peer(k, 1), device_id_type=MESH).start()
            return carry

        lax.fori_loop(k0, min(k1, n_slots - 1), go, 0)

    def all_of(src, dst, s, r, k0, k1):
        span = pl.ds(k0 * CAP, (min(k1, n_slots - 1) - k0) * CAP)
        return pltpu.make_async_remote_copy(src.at[span], dst.at[span], s, r, device_id=mate, device_id_type=MESH)

    def forward(c):
        k0, k1 = chunks[c]
        m, r0 = (k1 - k0) * CAP, k0 * CAP
        all_of(send, recv, ssem, rsem.at[c], k0, k1).wait_recv()
        if c == 0:
            w_copy.wait()
        got = recv[r0:r0 + m].reshape(m * QUARTERS, dq + fq)
        for q in range(QUARTERS):
            shape = (m, m * QUARTERS)
            sel = jnp.where(iota(shape, 0) * QUARTERS + q == iota(shape, 1), 1.0, 0.0).astype(BF16)
            part = dot(sel, got).astype(BF16)
            xbuf[r0:r0 + m, q * dq:(q + 1) * dq] = part[:, :dq]
            gbuf[r0:r0 + m, q * fq:(q + 1) * fq] = part[:, dq:]
        for n in range(f // ft):
            cols = slice(n * ft, (n + 1) * ft)
            pre = dot(xbuf[r0:r0 + m], wv[:, cols])
            sigma = jax.nn.sigmoid(pre)
            actbuf[r0:r0 + m, cols] = (pre * sigma).astype(BF16)
            gpbuf[r0:r0 + m, cols] = (
                gbuf[r0:r0 + m, cols].astype(F32) * sigma * (1.0 + pre * (1.0 - sigma))).astype(BF16)

    def give_back(c):
        k0, k1 = chunks[c]
        m, r0 = (k1 - k0) * CAP, k0 * CAP
        gp = gpbuf[r0:r0 + m]
        for q in range(QUARTERS):
            stk[q * m:(q + 1) * m, :dq] = dot(gp, wv[q * dq:(q + 1) * dq], ((1,), (1,))).astype(BF16)
            stk[q * m:(q + 1) * m, dq:] = actbuf[r0:r0 + m, q * fq:(q + 1) * fq]
        shape = (m * QUARTERS, m * QUARTERS)
        j = iota(shape, 1)
        jq = sum((j >= m * q).astype(jnp.int32) for q in range(1, QUARTERS))
        sel = jnp.where(iota(shape, 0) == (j - jq * m) * QUARTERS + jq, 1.0, 0.0).astype(BF16)
        packed = dot(sel, stk[:m * QUARTERS]).astype(BF16).reshape(m, QUARTERS, dq + fq)
        bsend[r0:r0 + m] = packed
        if k1 == n_slots:
            brecv[rows - CAP:] = packed[m - CAP:]

    def start_back(c):
        def back(k, carry):
            pltpu.make_async_remote_copy(
                slab(bsend, k), slab(brecv, k), bssem, brsem,
                device_id=plan.peer(k, -1), device_id_type=MESH).start()
            return carry

        lax.fori_loop(chunks[c][0], min(chunks[c][1], n_slots - 1), back, 0)

    last = len(chunks) - 1
    for c in range(last):
        forward(c)
        give_back(c)
        if EARLY:
            start_back(c)
    forward(last)
    if not EARLY:
        for c in range(last):
            start_back(c)

    groups = f // ft
    per = dq // half_rows
    owner = lambda i, h: (plan.y - i - 1 + 2 * ny) % ny if h == 0 else (plan.y + i + 1) % ny
    unit = lambda o, core, h: (o * 2 + core) * 2 + h
    far = (plan.dp, (plan.me + n_slots // 2) % n_slots)
    pairs, hops, swaps, out_copies = {}, {}, [], []

    labels = place_ref[...]
    lane = iota(labels.shape, 1)
    label = lambda s: jnp.sum(jnp.where(lane == s, labels, 0).astype(F32), axis=1, keepdims=True)
    same = jnp.where(label(plan.me) == label(far[1]), 1.0, 0.0)
    mask = jnp.broadcast_to(same, (half_rows, ft)) > 0.5

    def term(g):
        for q in range(QUARTERS):
            part = dot(xbuf[:, q * dq:(q + 1) * dq], gpbuf[:, g * ft:(g + 1) * ft], ((0,), (0,)))
            dw[g, q * per:(q + 1) * per] = part.astype(BF16).reshape(per, half_rows, ft)
        for i in range(ny):
            for h in range(2):
                cp = pltpu.make_async_remote_copy(
                    dw.at[g, unit(owner(i, h), 1 - plan.core, h)], pr.at[g, i, h], prs.at[g, i, h], prr.at[g, i, h],
                    device_id=mate, device_id_type=MESH)
                cp.start()
                pairs[g, i, h] = cp

    def hop(i, g):
        for h in range(2):
            u = unit(owner(i, h), plan.core, h)
            pairs[g, i, h].wait_recv()
            val = dw[g, u].astype(F32) + pr[g, i, h].astype(F32)
            if i > 0:
                hops[i - 1, g, h].wait_recv()
                val = val + rbuf[g, i - 1, h].astype(F32)
            if i < ny - 1:
                dw[g, u] = val.astype(BF16)
                cp = pltpu.make_async_remote_copy(
                    dw.at[g, u], rbuf.at[g, i, h], rss.at[g, i, h], rsr.at[g, i, h],
                    device_id=up if h == 0 else down, device_id_type=MESH)
                hops[i, g, h] = cp
            else:
                red[h, g] = val.astype(BF16)
                redm[h, g] = jnp.where(mask, val, 0.0).astype(BF16)
                out_copies.append(pltpu.make_async_copy(red.at[h, g], red_hbm.at[h, g], osem.at[2 + h * groups + g]))
                out_copies[-1].start()
                cp = pltpu.make_async_remote_copy(
                    redm.at[h, g], pbuf.at[h, g], ps.at[h, g], prv.at[h, g], device_id=far, device_id_type=MESH)
                swaps.append(cp)
            cp.start()

    term(0)
    for g in range(1, groups):
        term(g)
        hop(0, g - 1)
    hop(0, groups - 1)
    give_back(last)
    start_back(last)
    for i in range(1, ny):
        for g in range(groups):
            hop(i, g)

    all_of(bsend, brecv, bssem, brsem, 0, n_slots).wait_recv()
    back_rows = brecv[...].reshape(rows * QUARTERS, dq + fq)
    for q in range(QUARTERS):
        sel = jnp.where(iota((tok, rows * QUARTERS), 1) == place_col + q, 1.0, 0.0).astype(BF16)
        mine = dot(sel, back_rows)
        tg_ref[:, q * dq:(q + 1) * dq] = mine[:, :dq].astype(BF16)
        eo_ref[:, q * fq:(q + 1) * fq] = (rw * mine[:, dq:].astype(BF16).astype(F32)).astype(BF16)

    for i, (a, b) in enumerate(((eo_ref, eo_hbm), (tg_ref, tg_hbm))):
        out_copies.append(pltpu.make_async_copy(a, b, osem.at[i]))
        out_copies[-1].start()

    all_of(send, recv, ssem, rsem.at[0], 0, n_slots).wait_send()
    all_of(bsend, brecv, bssem, brsem, 0, n_slots).wait_send()
    for cp in pairs.values():
        cp.wait_send()
    for cp in hops.values():
        cp.wait_send()
    for cp in out_copies:
        cp.wait()
    for cp in swaps:
        cp.wait_send()
    for cp in swaps:
        cp.wait_recv()


def finish(
    eo_in, tg_in, red_in, pbuf_in, w_hbm, mom_hbm,
    eo_out, tg_out, nw_out, nm_out,
    redv, pbufv, wv, momv, nwv, nmv, isem, osem,
):
    dp = lax.axis_index("dp")
    _, groups, half, ft = redv.shape
    row0 = dp * 2 * half
    ins = {}
    for h in range(2):
        old = w_hbm.at[pl.ds(pl.multiple_of(row0 + h * half, 8), half)]
        for j, (a, b) in enumerate((
            (red_in.at[h], redv.at[h]), (pbuf_in.at[h], pbufv.at[h]), (mom_hbm.at[pl.ds(h * half, half)], momv.at[h]), (old, wv.at[h]))):
            ins[h, j] = pltpu.make_async_copy(a, b, isem.at[h, j])
            ins[h, j].start()
    outs = [pltpu.make_async_copy(a, b, osem.at[i]) for i, (a, b) in enumerate(((tg_in, tg_out), (eo_in, eo_out)))]
    for cp in outs:
        cp.start()
    for h in range(2):
        for j in range(4):
            ins[h, j].wait()
        for g in range(groups):
            cols = slice(g * ft, (g + 1) * ft)
            total = redv[h, g].astype(F32) + pbufv[h, g].astype(F32)
            fresh = (DECAY_RATE * momv[h, :, cols].astype(F32) + total).astype(BF16)
            nmv[h, :, cols] = fresh
            nwv[h, :, cols] = (wv[h, :, cols].astype(F32) - LEARNING_RATE * fresh.astype(F32)).astype(BF16)
        for j, (a, b) in enumerate(((nmv, nm_out), (nwv, nw_out))):
            outs.append(pltpu.make_async_copy(a.at[h], b.at[pl.ds(h * half, half)], osem.at[2 + h * 2 + j]))
            outs[-1].start()
    for cp in outs:
        cp.wait()


EARLY = False
CHUNKS = ((0, 24), (24, 48))


def shards(tokens, route_weight, cotangent, slot_ids, placement, weight, momentum):
    n_slots, n_dp = lax.axis_size("expert"), lax.axis_size("dp")
    tok, d = tokens.shape
    f = cotangent.shape[1]
    rows, ny = n_slots * CAP, n_dp // 2
    share = d // n_dp
    half, ft = share // 2, min(f, 256)
    groups = f // ft
    dq, fq = d // QUARTERS, f // QUARTERS
    chunks = CHUNKS if n_slots == 48 else ((0, n_slots // 2), (n_slots // 2, n_slots))
    cfg = dict(n_dp=n_dp, n_slots=n_slots, chunks=chunks, ftile=ft)
    vmem, dma = pltpu.VMEM, pltpu.SemaphoreType.DMA
    anywhere, in_hbm = pl.BlockSpec(memory_space=pl.ANY), pl.BlockSpec(memory_space=pltpu.HBM)
    slabs = (rows, QUARTERS, dq + fq)
    shape = jax.ShapeDtypeStruct
    pieces = shape((2, groups, half, ft), BF16)
    results = (shape((tok, f), BF16), shape((tok, d), BF16), shape((share, f), BF16), shape((share, f), BF16))
    eo, tg, red, partner = pl.pallas_call(
        functools.partial(body, cfg),
        out_shape=results[:2] + (pieces, pieces),
        in_specs=[in_hbm] * 6,
        out_specs=(anywhere,) * 4,
        scratch_shapes=[
            vmem((1, tok), jnp.int32), vmem((1, tok), F32), vmem((1, n_slots), jnp.int32),
            vmem((tok, d), BF16), vmem((tok, f), BF16), vmem((tok, f), BF16), vmem((tok, d), BF16),
            vmem((d, f), BF16),
            vmem((QUARTERS * max(rows, tok), dq + fq), BF16),
            vmem(slabs, BF16), vmem(slabs, BF16), vmem(slabs, BF16), vmem(slabs, BF16),
            vmem((rows, d), BF16),
            vmem((rows, f), BF16), vmem((rows, f), BF16), vmem((rows, f), BF16),
            vmem((groups, n_dp * 2, half, ft), BF16),
            vmem((groups, ny, 2, half, ft), BF16),
            vmem((groups, ny - 1, 2, half, ft), BF16),
            vmem((2, groups, half, ft), BF16), vmem((2, groups, half, ft), BF16),
            dma((5,)), dma, dma((2 + 2 * groups,)), dma, dma((len(chunks),)), dma, dma,
            dma((groups, ny, 2)), dma((groups, ny, 2)),
            dma((groups, ny - 1, 2)), dma((groups, ny - 1, 2)),
            dma((2, groups)), dma((2, groups)),
        ],
        compiler_params=pltpu.CompilerParams(
            collective_id=0, has_side_effects=True, vmem_limit_bytes=48 * 1024 * 1024),
    )(slot_ids[None, :], route_weight[None, :], placement[None, :], tokens, cotangent, weight[0])
    eo, tg, nw, nm = pl.pallas_call(
        finish,
        out_shape=results,
        in_specs=[anywhere] * 4 + [in_hbm, anywhere],
        out_specs=(in_hbm,) * 4,
        scratch_shapes=[
            vmem((2, groups, half, ft), BF16), vmem((2, groups, half, ft), BF16),
            vmem((2, half, f), BF16), vmem((2, half, f), BF16), vmem((2, half, f), BF16), vmem((2, half, f), BF16),
            dma((2, 4)), dma((6,)),
        ],
        compiler_params=pltpu.CompilerParams(vmem_limit_bytes=12 * 1024 * 1024),
    )(eo, tg, red, partner, weight[0], momentum[0])
    return eo, tg, nw[None], nm[None]


def solution(mesh):
    return jax.shard_map(
        shards,
        mesh=mesh,
        in_specs=(
            P(("dp", "expert"), None),
            P(("dp", "expert")),
            P(("dp", "expert"), None),
            P(("dp", "expert")),
            P(),
            P("expert", None, None),
            P("expert", "dp", None),
        ),
        out_specs=(
            P(("dp", "expert"), None),
            P(("dp", "expert"), None),
            P("expert", "dp", None),
            P("expert", "dp", None),
        ),
        check_vma=False,
    )
```

```python
import functools

import jax
import jax.numpy as jnp
from jax import lax
from jax.experimental import pallas as pl
from jax.experimental.pallas import tpu as pltpu
from jax.sharding import PartitionSpec as P

LEARNING_RATE = 0.004
DECAY_RATE = 0.9
CAP = 3
QUARTERS = 4
MESH = pl.DeviceIdType.MESH
F32, BF16 = jnp.float32, jnp.bfloat16


def dot(a, b, dims=((1,), (0,))):
    return lax.dot_general(a, b, (dims, ((), ())), preferred_element_type=F32)


def iota(shape, axis):
    return lax.broadcasted_iota(jnp.int32, shape, axis)


class Plan:
    def __init__(self, n_dp, n_slots):
        self.nz, self.nx = (12, 4) if n_slots == 48 else (n_slots // 2, 2)
        self.ny = n_dp // 2
        self.n_slots, self.n_dp = n_slots, n_dp
        self.dp, self.me = lax.axis_index("dp"), lax.axis_index("expert")
        self.y, self.core = self.dp // 2, self.dp % 2
        self.z, self.x = self.me // self.nx, self.me % self.nx
        self.sign = 1 - 2 * self.core

    def shift(self, k):
        f = self.nz - 1 - k // self.nx
        dz = (f % 2) * ((f + 1) // 2) + (1 - f % 2) * (self.nz - f // 2)
        dx = self.nx - 1 - k % self.nx
        return dz, dx

    def peer(self, k, way):
        dz, dx = self.shift(k)
        z = (self.z + way * self.sign * dz + 2 * self.nz) % self.nz
        x = (self.x + way * self.sign * dx + 2 * self.nx) % self.nx
        return self.dp, z * self.nx + x

    def visit(self, slot):
        zs, xs = slot // self.nx, slot % self.nx
        dz = (self.sign * (zs - self.z) + 2 * self.nz) % self.nz
        dx = (self.sign * (xs - self.x) + 2 * self.nx) % self.nx
        f = jnp.where(dz == 0, 0, jnp.where(dz <= self.nz // 2, 2 * dz - 1, 2 * (self.nz - dz)))
        return (self.nz - 1 - f) * self.nx + (self.nx - 1 - dx)


def body(
    cfg,
    slot_hbm, rw_hbm, place_hbm, tok_hbm, cot_hbm, w_hbm,
    eo_hbm, tg_hbm, red_hbm, pbuf,
    slot_ref, rw_ref, place_ref, tok_ref, cot_ref, eo_ref, tg_ref,
    wv, stk, send, recv, bsend, brecv, xbuf, gbuf, gpbuf, actbuf, dw, pr, rbuf, red, redm,
    isem, wsem, osem, ssem, rsem, bssem, brsem, prs, prr, rss, rsr, ps, prv,
):
    plan = Plan(cfg["n_dp"], cfg["n_slots"])
    n_slots, ny = plan.n_slots, plan.ny
    tok, d = tok_ref.shape
    f = cot_ref.shape[1]
    dq, fq = d // QUARTERS, f // QUARTERS
    rows = n_slots * CAP
    chunks = cfg["chunks"]
    ft = cfg["ftile"]
    half_rows = dw.shape[2]

    barrier = pltpu.get_barrier_semaphore()

    def greet(k, c):
        pl.semaphore_signal(barrier, inc=1, device_id=plan.peer(k, 1), device_id_type=MESH)
        return c

    lax.fori_loop(0, n_slots - 1, greet, 0)
    up = (((plan.y + 1) % ny) * 2 + plan.core, plan.me)
    down = (((plan.y + ny - 1) % ny) * 2 + plan.core, plan.me)
    mate = (plan.y * 2 + 1 - plan.core, plan.me)
    for dev in (up, down, mate):
        pl.semaphore_signal(barrier, inc=1, device_id=dev, device_id_type=MESH)

    loads = [
        pltpu.make_async_copy(a, b, isem.at[i])
        for i, (a, b) in enumerate(
            ((slot_hbm, slot_ref), (rw_hbm, rw_ref), (place_hbm, place_ref), (tok_hbm, tok_ref), (cot_hbm, cot_ref)))
    ]
    for cp in loads:
        cp.start()
    w_copy = pltpu.make_async_copy(w_hbm, wv, wsem)
    w_copy.start()
    for cp in loads[:3]:
        cp.wait()

    srow = slot_ref[...]
    hot = (iota((n_slots, tok), 0) == srow).astype(F32)
    tri = (iota((tok, tok), 0) <= iota((tok, tok), 1)).astype(BF16)
    rank = jnp.sum(hot * (dot(hot.astype(BF16), tri) - 1.0), axis=0, keepdims=True)
    place_row = (plan.visit(srow) * CAP + rank.astype(jnp.int32)) * QUARTERS
    diag = iota((tok, tok), 0) == iota((tok, tok), 1)
    upright = lambda row: jnp.sum(jnp.where(diag, row, 0.0), axis=1, keepdims=True)
    place_col = upright(place_row.astype(F32)).astype(jnp.int32)
    rw = upright(rw_ref[...])
    for cp in loads[3:]:
        cp.wait()
    for q in range(QUARTERS):
        stk[q * tok:(q + 1) * tok, :dq] = tok_ref[:, q * dq:(q + 1) * dq]
        stk[q * tok:(q + 1) * tok, dq:] = (rw * cot_ref[:, q * fq:(q + 1) * fq].astype(F32)).astype(BF16)
    want = jnp.concatenate([place_row + q for q in range(QUARTERS)], axis=1)
    pick = jnp.where(iota((rows * QUARTERS, QUARTERS * tok), 0) == want, 1.0, 0.0).astype(BF16)
    packed = dot(pick, stk[:QUARTERS * tok]).astype(BF16).reshape(rows, QUARTERS, dq + fq)
    send[...] = packed
    recv[rows - CAP:] = packed[rows - CAP:]

    pl.semaphore_wait(barrier, n_slots - 1 + 3)

    def slab(ref, k):
        return ref.at[pl.ds(k * CAP, CAP)]

    for c, (k0, k1) in enumerate(chunks):
        def go(k, carry, c=c):
            pltpu.make_async_remote_copy(
                slab(send, k), slab(recv, k), ssem, rsem.at[c],
                device_id=plan.peer(k, 1), device_id_type=MESH).start()
            return carry

        lax.fori_loop(k0, min(k1, n_slots - 1), go, 0)

    def all_of(src, dst, s, r, k0, k1):
        span = pl.ds(k0 * CAP, (min(k1, n_slots - 1) - k0) * CAP)
        return pltpu.make_async_remote_copy(src.at[span], dst.at[span], s, r, device_id=mate, device_id_type=MESH)

    def forward(c):
        k0, k1 = chunks[c]
        m, r0 = (k1 - k0) * CAP, k0 * CAP
        all_of(send, recv, ssem, rsem.at[c], k0, k1).wait_recv()
        if c == 0:
            w_copy.wait()
        got = recv[r0:r0 + m].reshape(m * QUARTERS, dq + fq)
        for q in range(QUARTERS):
            shape = (m, m * QUARTERS)
            sel = jnp.where(iota(shape, 0) * QUARTERS + q == iota(shape, 1), 1.0, 0.0).astype(BF16)
            part = dot(sel, got).astype(BF16)
            xbuf[r0:r0 + m, q * dq:(q + 1) * dq] = part[:, :dq]
            gbuf[r0:r0 + m, q * fq:(q + 1) * fq] = part[:, dq:]
        for n in range(f // ft):
            cols = slice(n * ft, (n + 1) * ft)
            pre = dot(xbuf[r0:r0 + m], wv[:, cols])
            sigma = jax.nn.sigmoid(pre)
            actbuf[r0:r0 + m, cols] = (pre * sigma).astype(BF16)
            gpbuf[r0:r0 + m, cols] = (
                gbuf[r0:r0 + m, cols].astype(F32) * sigma * (1.0 + pre * (1.0 - sigma))).astype(BF16)

    def give_back(c):
        k0, k1 = chunks[c]
        m, r0 = (k1 - k0) * CAP, k0 * CAP
        gp = gpbuf[r0:r0 + m]
        for q in range(QUARTERS):
            stk[q * m:(q + 1) * m, :dq] = dot(gp, wv[q * dq:(q + 1) * dq], ((1,), (1,))).astype(BF16)
            stk[q * m:(q + 1) * m, dq:] = actbuf[r0:r0 + m, q * fq:(q + 1) * fq]
        shape = (m * QUARTERS, m * QUARTERS)
        j = iota(shape, 1)
        jq = sum((j >= m * q).astype(jnp.int32) for q in range(1, QUARTERS))
        sel = jnp.where(iota(shape, 0) == (j - jq * m) * QUARTERS + jq, 1.0, 0.0).astype(BF16)
        packed = dot(sel, stk[:m * QUARTERS]).astype(BF16).reshape(m, QUARTERS, dq + fq)
        bsend[r0:r0 + m] = packed
        if k1 == n_slots:
            brecv[rows - CAP:] = packed[m - CAP:]

    def start_back(c):
        def back(k, carry):
            pltpu.make_async_remote_copy(
                slab(bsend, k), slab(brecv, k), bssem, brsem,
                device_id=plan.peer(k, -1), device_id_type=MESH).start()
            return carry

        lax.fori_loop(chunks[c][0], min(chunks[c][1], n_slots - 1), back, 0)

    last = len(chunks) - 1
    for c in range(last):
        forward(c)
        give_back(c)
        if EARLY:
            start_back(c)
    forward(last)
    if not EARLY:
        for c in range(last):
            start_back(c)

    groups = f // ft
    per = dq // half_rows
    owner = lambda i, h: (plan.y - i - 1 + 2 * ny) % ny if h == 0 else (plan.y + i + 1) % ny
    unit = lambda o, core, h: (o * 2 + core) * 2 + h
    far = (plan.dp, (plan.me + n_slots // 2) % n_slots)
    pairs, hops, swaps, out_copies = {}, {}, [], []

    labels = place_ref[...]
    lane = iota(labels.shape, 1)
    label = lambda s: jnp.sum(jnp.where(lane == s, labels, 0).astype(F32), axis=1, keepdims=True)
    same = jnp.where(label(plan.me) == label(far[1]), 1.0, 0.0)
    mask = jnp.broadcast_to(same, (half_rows, ft)) > 0.5

    def term(g):
        for q in range(QUARTERS):
            part = dot(xbuf[:, q * dq:(q + 1) * dq], gpbuf[:, g * ft:(g + 1) * ft], ((0,), (0,)))
            dw[g, q * per:(q + 1) * per] = part.astype(BF16).reshape(per, half_rows, ft)
        for i in range(ny):
            for h in range(2):
                cp = pltpu.make_async_remote_copy(
                    dw.at[g, unit(owner(i, h), 1 - plan.core, h)], pr.at[g, i, h], prs.at[g, i, h], prr.at[g, i, h],
                    device_id=mate, device_id_type=MESH)
                cp.start()
                pairs[g, i, h] = cp

    def hop(i, g):
        for h in range(2):
            u = unit(owner(i, h), plan.core, h)
            pairs[g, i, h].wait_recv()
            val = dw[g, u].astype(F32) + pr[g, i, h].astype(F32)
            if i > 0:
                hops[i - 1, g, h].wait_recv()
                val = val + rbuf[g, i - 1, h].astype(F32)
            if i < ny - 1:
                dw[g, u] = val.astype(BF16)
                cp = pltpu.make_async_remote_copy(
                    dw.at[g, u], rbuf.at[g, i, h], rss.at[g, i, h], rsr.at[g, i, h],
                    device_id=up if h == 0 else down, device_id_type=MESH)
                hops[i, g, h] = cp
            else:
                red[h, g] = val.astype(BF16)
                redm[h, g] = jnp.where(mask, val, 0.0).astype(BF16)
                out_copies.append(pltpu.make_async_copy(red.at[h, g], red_hbm.at[h, g], osem.at[2 + h * groups + g]))
                out_copies[-1].start()
                cp = pltpu.make_async_remote_copy(
                    redm.at[h, g], pbuf.at[h, g], ps.at[h, g], prv.at[h, g], device_id=far, device_id_type=MESH)
                swaps.append(cp)
            cp.start()

    term(0)
    for g in range(1, groups):
        term(g)
        hop(0, g - 1)
    hop(0, groups - 1)
    give_back(last)
    start_back(last)
    for i in range(1, ny):
        for g in range(groups):
            hop(i, g)

    all_of(bsend, brecv, bssem, brsem, 0, n_slots).wait_recv()
    back_rows = brecv[...].reshape(rows * QUARTERS, dq + fq)
    for q in range(QUARTERS):
        sel = jnp.where(iota((tok, rows * QUARTERS), 1) == place_col + q, 1.0, 0.0).astype(BF16)
        mine = dot(sel, back_rows)
        tg_ref[:, q * dq:(q + 1) * dq] = mine[:, :dq].astype(BF16)
        eo_ref[:, q * fq:(q + 1) * fq] = (rw * mine[:, dq:].astype(BF16).astype(F32)).astype(BF16)

    for i, (a, b) in enumerate(((eo_ref, eo_hbm), (tg_ref, tg_hbm))):
        out_copies.append(pltpu.make_async_copy(a, b, osem.at[i]))
        out_copies[-1].start()

    all_of(send, recv, ssem, rsem.at[0], 0, n_slots).wait_send()
    all_of(bsend, brecv, bssem, brsem, 0, n_slots).wait_send()
    for cp in pairs.values():
        cp.wait_send()
    for cp in hops.values():
        cp.wait_send()
    for cp in out_copies:
        cp.wait()
    for cp in swaps:
        cp.wait_send()
    for cp in swaps:
        cp.wait_recv()


def finish(
    eo_in, tg_in, red_in, pbuf_in, w_hbm, mom_hbm,
    eo_out, tg_out, nw_out, nm_out,
    eov, tgv, redv, pbufv, wv, momv, nwv, nmv, isem, tsem, osem,
):
    dp = lax.axis_index("dp")
    _, groups, half, ft = redv.shape
    row0 = dp * 2 * half
    ins = {}
    for h in range(2):
        old = w_hbm.at[pl.ds(pl.multiple_of(row0 + h * half, 8), half)]
        for j, (a, b) in enumerate((
            (red_in.at[h], redv.at[h]), (pbuf_in.at[h], pbufv.at[h]), (mom_hbm.at[pl.ds(h * half, half)], momv.at[h]), (old, wv.at[h]))):
            ins[h, j] = pltpu.make_async_copy(a, b, isem.at[h, j])
            ins[h, j].start()
    whole = [pltpu.make_async_copy(a, b, tsem.at[i]) for i, (a, b) in enumerate(((tg_in, tgv), (eo_in, eov)))]
    for cp in whole:
        cp.start()
    outs = [pltpu.make_async_copy(a, b, osem.at[i]) for i, (a, b) in enumerate(((tgv, tg_out), (eov, eo_out)))]
    for h in range(2):
        for j in range(4):
            ins[h, j].wait()
        for g in range(groups):
            cols = slice(g * ft, (g + 1) * ft)
            total = redv[h, g].astype(F32) + pbufv[h, g].astype(F32)
            fresh = (DECAY_RATE * momv[h, :, cols].astype(F32) + total).astype(BF16)
            nmv[h, :, cols] = fresh
            nwv[h, :, cols] = (wv[h, :, cols].astype(F32) - LEARNING_RATE * fresh.astype(F32)).astype(BF16)
        for j, (a, b) in enumerate(((nmv, nm_out), (nwv, nw_out))):
            outs.append(pltpu.make_async_copy(a.at[h], b.at[pl.ds(h * half, half)], osem.at[2 + h * 2 + j]))
            outs[-1].start()
        if h == 0:
            for i in range(2):
                whole[i].wait()
                outs[i].start()
    for cp in outs:
        cp.wait()


EARLY = False
CHUNKS = ((0, 24), (24, 48))


def shards(tokens, route_weight, cotangent, slot_ids, placement, weight, momentum):
    n_slots, n_dp = lax.axis_size("expert"), lax.axis_size("dp")
    tok, d = tokens.shape
    f = cotangent.shape[1]
    rows, ny = n_slots * CAP, n_dp // 2
    share = d // n_dp
    half, ft = share // 2, min(f, 256)
    groups = f // ft
    dq, fq = d // QUARTERS, f // QUARTERS
    chunks = CHUNKS if n_slots == 48 else ((0, n_slots // 2), (n_slots // 2, n_slots))
    cfg = dict(n_dp=n_dp, n_slots=n_slots, chunks=chunks, ftile=ft)
    vmem, dma = pltpu.VMEM, pltpu.SemaphoreType.DMA
    anywhere = pl.BlockSpec(memory_space=pl.ANY)
    slabs = (rows, QUARTERS, dq + fq)
    shape = jax.ShapeDtypeStruct
    pieces = shape((2, groups, half, ft), BF16)
    results = (shape((tok, f), BF16), shape((tok, d), BF16), shape((share, f), BF16), shape((share, f), BF16))
    eo, tg, red, partner = pl.pallas_call(
        functools.partial(body, cfg),
        out_shape=results[:2] + (pieces, pieces),
        in_specs=[anywhere] * 6,
        out_specs=(anywhere,) * 4,
        scratch_shapes=[
            vmem((1, tok), jnp.int32), vmem((1, tok), F32), vmem((1, n_slots), jnp.int32),
            vmem((tok, d), BF16), vmem((tok, f), BF16), vmem((tok, f), BF16), vmem((tok, d), BF16),
            vmem((d, f), BF16),
            vmem((QUARTERS * max(rows, tok), dq + fq), BF16),
            vmem(slabs, BF16), vmem(slabs, BF16), vmem(slabs, BF16), vmem(slabs, BF16),
            vmem((rows, d), BF16),
            vmem((rows, f), BF16), vmem((rows, f), BF16), vmem((rows, f), BF16),
            vmem((groups, n_dp * 2, half, ft), BF16),
            vmem((groups, ny, 2, half, ft), BF16),
            vmem((groups, ny - 1, 2, half, ft), BF16),
            vmem((2, groups, half, ft), BF16), vmem((2, groups, half, ft), BF16),
            dma((5,)), dma, dma((2 + 2 * groups,)), dma, dma((len(chunks),)), dma, dma,
            dma((groups, ny, 2)), dma((groups, ny, 2)),
            dma((groups, ny - 1, 2)), dma((groups, ny - 1, 2)),
            dma((2, groups)), dma((2, groups)),
        ],
        compiler_params=pltpu.CompilerParams(
            collective_id=0, has_side_effects=True, vmem_limit_bytes=60 * 1024 * 1024),
    )(slot_ids[None, :], route_weight[None, :], placement[None, :], tokens, cotangent, weight[0])
    eo, tg, nw, nm = pl.pallas_call(
        finish,
        out_shape=results,
        in_specs=[anywhere] * 6,
        out_specs=(anywhere,) * 4,
        scratch_shapes=[
            vmem((tok, f), BF16), vmem((tok, d), BF16), vmem((2, groups, half, ft), BF16), vmem((2, groups, half, ft), BF16),
            vmem((2, half, f), BF16), vmem((2, half, f), BF16), vmem((2, half, f), BF16), vmem((2, half, f), BF16),
            dma((2, 4)), dma((2,)), dma((6,)),
        ],
    )(eo, tg, red, partner, weight[0], momentum[0])
    return eo, tg, nw[None], nm[None]


def solution(mesh):
    return jax.shard_map(
        shards,
        mesh=mesh,
        in_specs=(
            P(("dp", "expert"), None),
            P(("dp", "expert")),
            P(("dp", "expert"), None),
            P(("dp", "expert")),
            P(),
            P("expert", None, None),
            P("expert", "dp", None),
        ),
        out_specs=(
            P(("dp", "expert"), None),
            P(("dp", "expert"), None),
            P("expert", "dp", None),
            P("expert", "dp", None),
        ),
        check_vma=False,
    )
```
